32 devices in a mesh: section: 2 (over core), seq: 4 (over y, x), tensor: 4 (over z).
Axes of the slice: x: 2, y: 2, z: 4, core: 2. Of those that a mesh axis runs over, the one named last changes fastest.
Arguments:
- tokens: bfloat16 [4096, 1024], P('seq', 'tensor'), may hold values from -6 to 6
- segments: int32 [8, 512], P('seq'), may hold values from 0 to 3, never falling along the last dimension, each value on 1 to 256 neighbouring positions
- cotangent: bfloat16 [4096, 1024], P('seq', 'tensor'), may hold values from -6 to 6
- norm1_gain: bfloat16 [2, 1024], P('section', ('tensor', 'seq')), may hold values from 0.5 to 1.5
- norm1_bias: bfloat16 [2, 1024], P('section', ('tensor', 'seq')), may hold values from -3 to 3
- qkv_weight: bfloat16 [2, 1024, 16, 192], P('section', 'seq', 'tensor'), may hold values from -0.1875 to 0.1875
- qv_bias: bfloat16 [2, 16, 128], P('section', 'tensor', 'seq'), may hold values from -4 to 4
- out_weight: bfloat16 [2, 16, 64, 1024], P('section', 'tensor', None, 'seq'), may hold values from -0.75 to 0.75
- out_bias: bfloat16 [2, 1024], P('section', ('tensor', 'seq')), may hold values from -3 to 3
- norm2_gain: bfloat16 [2, 1024], P('section', ('tensor', 'seq')), may hold values from 0.5 to 1.5
- norm2_bias: bfloat16 [2, 1024], P('section', ('tensor', 'seq')), may hold values from -3 to 3
- up_weight: bfloat16 [2, 1024, 4096], P('section', 'seq', 'tensor'), may hold values from -0.1875 to 0.1875
- up_bias: bfloat16 [2, 4096], P('section', ('tensor', 'seq')), may hold values from -4 to 4
- down_weight: bfloat16 [2, 4096, 1024], P('section', 'tensor', 'seq'), may hold values from -0.09375 to 0.09375
- down_bias: bfloat16 [2, 1024], P('section', ('tensor', 'seq')), may hold values from -3 to 3
Outputs:
- section_out: bfloat16 [2, 4096, 1024], P('section', 'seq', 'tensor')
- input_grad: bfloat16 [2, 4096, 1024], P('section', 'seq', 'tensor')
- grad_norm1_gain: float32 [2, 1024], P('section', ('tensor', 'seq'))
- grad_norm1_bias: float32 [2, 1024], P('section', ('tensor', 'seq'))
- grad_qkv_weight: float32 [2, 1024, 16, 192], P('section', 'seq', 'tensor')
- grad_qv_bias: float32 [2, 16, 128], P('section', 'tensor', 'seq')
- grad_out_weight: float32 [2, 16, 64, 1024], P('section', 'tensor', None, 'seq')
- grad_out_bias: float32 [2, 1024], P('section', ('tensor', 'seq'))
- grad_norm2_gain: float32 [2, 1024], P('section', ('tensor', 'seq'))
- grad_norm2_bias: float32 [2, 1024], P('section', ('tensor', 'seq'))
- grad_up_weight: float32 [2, 1024, 4096], P('section', 'seq', 'tensor')
- grad_up_bias: float32 [2, 4096], P('section', ('tensor', 'seq'))
- grad_down_weight: float32 [2, 4096, 1024], P('section', 'tensor', 'seq')
- grad_down_bias: float32 [2, 1024], P('section', ('tensor', 'seq'))
The draws below stay inside these ranges and needn't reach their ends.
Inputs may be any that keep to these rules, and one draw needn't show every extreme that they name: `segments`: along each sequence the document numbers never fall; every document holds 1 to 256 positions.
All inputs are finite; a program needn't handle non-finite values.
Results may differ from the reference program's by a relative error of at most 0.02.
Values may be sent and summed in bfloat16 or wider, within the bound.
A program may use at most 192 MiB of HBM per device.

```python
import math
import jax
import jax.numpy as jnp
import numpy as np
from jax import lax

D = 1024
H = 16
HD = 64
FF = 4096
LEN = 512
DOCS = 4
LAYERS = 2
SEQS = 8
TOKENS = 4096


def level_of(own_key, extent, split, smallest, high):
    def one(axis_at, shards_of):
        heights = jax.random.uniform(jax.random.fold_in(jax.random.fold_in(own_key, 6), axis_at), (shards_of,), jnp.float32, smallest / len(split), high / len(split))
        return jnp.repeat(jnp.exp(heights), extent[axis_at] // shards_of).reshape((-1,) + (1,) * (len(extent) - axis_at - 1))

    loudness = one(*split[0])
    for cut in split[1:]:
        loudness = loudness * one(*cut)
    return loudness


def split_up(count, total, most, skew):
    weights = [(1 << 20) // math.isqrt(standing ** skew) + 1 for standing in range(2, count + 1)]
    spare, counts = total - most - (count - 1), [1] * (count - 1)
    while spare > 0:
        free = [i for i in range(count - 1) if counts[i] < most]
        mass, remaining = sum([weights[i] for i in free]), spare
        for i in free:
            addition = min(most - counts[i], max(1, remaining * weights[i] // mass), spare)
            counts[i] = counts[i] + addition
            spare = spare - addition
    return np.array([most] + counts)


def ragged_sizes(rng, number_of, total, most, lean):
    if number_of == 2:
        one = jax.random.randint(rng, (), max(1, total - most), min(most, total - 1) + 1)
        return jnp.stack([one, total - one])
    sizes = jnp.asarray(split_up(number_of, total, most, lean), jnp.int32)
    twos = (number_of - 1) // 2
    donor, taker = sizes[1:1 + 2 * twos:2], sizes[2:2 + 2 * twos:2]
    margin = jnp.minimum(donor - 1, most - taker)
    passed = jax.random.randint(jax.random.fold_in(rng, 1), (twos,), 0, 1 << 20) % (margin + 1)
    sizes = sizes.at[1:1 + 2 * twos:2].set(donor - passed).at[2:2 + 2 * twos:2].set(taker + passed)
    return sizes[jax.random.permutation(jax.random.fold_in(rng, 2), number_of)]


def normal_values(key, shape, spread, most, cuts=(), kind=jnp.bfloat16):
    drawn = spread * jax.random.normal(key, shape, jnp.float32)
    if cuts:
        drawn = drawn * level_of(key, shape, cuts, -0.22, 0.18)
    return jnp.clip(drawn, -most, most).astype(kind)


def setup_inputs(seed: int = 0) -> dict:
    key_list = jax.random.split(jax.random.key(seed), 16)
    tokens = normal_values(key_list[0], (TOKENS, D), 1.0, 6.0, ((0, 4), (1, 4)))
    segments = jax.vmap(lambda own: jnp.searchsorted(jnp.cumsum(ragged_sizes(own, DOCS, LEN, LEN // 2, 1)), jnp.arange(LEN), side="right"))(jax.random.split(key_list[1], SEQS)).reshape((SEQS, LEN)).astype(jnp.int32)
    cotangent = normal_values(key_list[2], (TOKENS, D), 1.0, 6.0, ((0, 4), (1, 4)))
    norm1_gain = jnp.clip(1.0 + 0.1 * jax.random.normal(key_list[3], (LAYERS, D), jnp.float32), 0.5, 1.5).astype(jnp.bfloat16)
    norm1_bias = normal_values(key_list[4], (LAYERS, D), 0.3, 3.0, ((0, 2), (1, 16)))
    qkv_weight = normal_values(key_list[5], (LAYERS, D, H, 3 * HD), D ** -0.5, 0.1875, ((0, 2), (1, 4), (2, 4)))
    qv_bias = normal_values(key_list[6], (LAYERS, H, 2 * HD), 0.5, 4.0, ((0, 2), (1, 4), (2, 4)))
    out_weight = normal_values(key_list[7], (LAYERS, H, HD, D), (D // 16) ** -0.5, 0.75, ((0, 2), (1, 4), (3, 4)))
    out_bias = normal_values(key_list[8], (LAYERS, D), 0.3, 3.0, ((0, 2), (1, 16)))
    norm2_gain = jnp.clip(1.0 + 0.1 * jax.random.normal(key_list[9], (LAYERS, D), jnp.float32), 0.5, 1.5).astype(jnp.bfloat16)
    norm2_bias = normal_values(key_list[10], (LAYERS, D), 0.3, 3.0, ((0, 2), (1, 16)))
    up_weight = normal_values(key_list[11], (LAYERS, D, FF), D ** -0.5, 0.1875, ((0, 2), (1, 4), (2, 4)))
    up_bias = normal_values(key_list[12], (LAYERS, FF), 0.5, 4.0, ((0, 2), (1, 16)))
    down_weight = normal_values(key_list[13], (LAYERS, FF, D), FF ** -0.5, 0.09375, ((0, 2), (1, 4), (2, 4)))
    down_bias = normal_values(key_list[14], (LAYERS, D), 0.3, 3.0, ((0, 2), (1, 16)))
    return {"tokens": tokens, "segments": segments, "cotangent": cotangent, "norm1_gain": norm1_gain, "norm1_bias": norm1_bias, "qkv_weight": qkv_weight, "qv_bias": qv_bias, "out_weight": out_weight, "out_bias": out_bias, "norm2_gain": norm2_gain, "norm2_bias": norm2_bias, "up_weight": up_weight, "up_bias": up_bias, "down_weight": down_weight, "down_bias": down_bias}


@jax.custom_vjp
def low(v):
    return lax.optimization_barrier(v.astype(jnp.bfloat16)).astype(jnp.float32)

@jax.custom_vjp
def low_back(v):
    return v

def low_keep(v):
    return (low(v), None)

def low_pass(kept, grad):
    return (grad,)

def back_keep(v):
    return (v, None)

def back_low(kept, grad):
    return (low(grad),)
low.defvjp(low_keep, low_pass)
low_back.defvjp(back_keep, back_low)
epsilon = 1e-05
highest = lax.Precision.HIGHEST

def layer_norm(value, gain, shift):
    average = lax.optimization_barrier(jnp.mean(value, axis=-1, keepdims=True))
    variance = lax.optimization_barrier(jnp.mean(value * value, axis=-1, keepdims=True)) - average * average
    return (value - average) * lax.rsqrt(variance + epsilon) * gain + shift

def attend_one(query, keys, values, segment):
    factor = 1.0 / math.sqrt(HD)
    scores = low_back(jnp.einsum('qhe,khe->hqk', query, keys, precision=highest) * factor)
    place = jnp.arange(LEN)
    allowed = (place[None, :] <= place[:, None]) & (segment[:, None] == segment[None, :])
    masked = jnp.where(allowed[None], scores, -1e+30)
    highest_score = lax.optimization_barrier(jnp.max(masked, axis=-1, keepdims=True))
    raised = jnp.exp(masked - highest_score)
    chance = low(raised / lax.optimization_barrier(jnp.sum(raised, axis=-1, keepdims=True)))
    return jnp.einsum('hqk,khe->qhe', chance, values, precision=highest)

def layer(inputs, segs, params):
    gain1, bias1, w_qkv, b_qv, w_out, b_out, gain2, bias2, w_up, b_up, w_down, b_down = params
    rows = low_back(inputs)
    normed = low(layer_norm(rows, gain1, bias1))
    mixed = jnp.einsum('nd,dhe->nhe', normed, w_qkv, precision=highest)
    query = low(low_back(mixed[..., :HD] + b_qv[:, :HD]))
    keys = low(low_back(mixed[..., HD:2 * HD]))
    values = low(low_back(mixed[..., 2 * HD:] + b_qv[:, HD:]))
    count = rows.shape[0] // LEN
    shape4 = (count, LEN, H, HD)
    attend_saved = jax.checkpoint(attend_one)

    def one_sequence(item):
        return attend_saved(item[0], item[1], item[2], item[3])
    context = lax.map(one_sequence, (query.reshape(shape4), keys.reshape(shape4), values.reshape(shape4), segs))
    context = low(low_back(context.reshape(rows.shape[0], H * HD)))
    attn = low_back(jnp.dot(context, w_out.reshape(H * HD, D), precision=highest) + b_out)
    hidden = rows + attn
    normed2 = low(layer_norm(hidden, gain2, bias2))
    upper = low_back(jnp.dot(normed2, w_up, precision=highest) + b_up)
    active = low(jax.nn.gelu(upper, approximate=True))
    branch = low_back(jnp.dot(active, w_down, precision=highest) + b_down)
    return low(hidden + branch)

def reference(tokens, segments, cotangent, norm1_gain, norm1_bias, qkv_weight, qv_bias, out_weight, out_bias, norm2_gain, norm2_bias, up_weight, up_bias, down_weight, down_bias):
    params = (norm1_gain, norm1_bias, qkv_weight, qv_bias, out_weight, out_bias, norm2_gain, norm2_bias, up_weight, up_bias, down_weight, down_bias)
    params = tuple((item.astype(jnp.float32) for item in params))
    first = tuple((item[0] for item in params))
    second = tuple((item[1] for item in params))
    group = math.gcd(SEQS, 8)
    count = SEQS // group
    blocks = tokens.astype(jnp.float32).reshape(count, group * LEN, D)
    backs = cotangent.astype(jnp.float32).reshape(count, group * LEN, D)
    segs_all = segments.reshape(count, group, LEN)

    def step(carry, item):
        block, segs, back = item

        def section_fn(value, weights):
            return layer(value, segs, weights)
        middle, pull_first = jax.vjp(section_fn, block, first)
        final, pull_second = jax.vjp(section_fn, middle, second)
        grad_middle, grad_second = pull_second(back)
        grad_block, grad_first = pull_first(grad_middle)
        total_first = jax.tree.map(lambda acc, new: acc + new, carry[0], grad_first)
        total_second = jax.tree.map(lambda acc, new: acc + new, carry[1], grad_second)
        return ((total_first, total_second), (middle, final, grad_block, grad_middle))
    start = (jax.tree.map(jnp.zeros_like, first), jax.tree.map(jnp.zeros_like, second))
    totals, stacked = lax.scan(step, start, (blocks, segs_all, backs))
    middle, final, grad_block, grad_middle = (item.reshape(TOKENS, D) for item in stacked)
    section_out = jnp.stack([middle, final]).astype(jnp.bfloat16)
    input_grad = jnp.stack([grad_block, grad_middle]).astype(jnp.bfloat16)
    grads = tuple((jnp.stack([one, two]) for one, two in zip(totals[0], totals[1])))
    return (section_out, input_grad, grads[0], grads[1], grads[2], grads[3], grads[4], grads[5], grads[6], grads[7], grads[8], grads[9], grads[10], grads[11])
```

```python
import functools
import math

import jax
import jax.numpy as jnp
from jax import lax
from jax.sharding import PartitionSpec as P

epsilon = 1e-05
floor_value = -1e30
f32 = jnp.float32
bf16 = jnp.bfloat16


def gather_columns(piece):
    return lax.all_gather(piece, "tensor", axis=1, tiled=True)


def gather_rows(piece):
    return lax.all_gather(piece, "tensor", axis=0, tiled=True)


def scatter_rows(partial_rows):
    return lax.psum_scatter(
        partial_rows.astype(bf16), "tensor", scatter_dimension=0, tiled=True
    ).astype(f32)


def norm_parts(rows):
    average = jnp.mean(rows, axis=1, keepdims=True)
    variance = jnp.mean(rows * rows, axis=1, keepdims=True) - average * average
    scale = lax.rsqrt(variance + epsilon)
    return ((rows - average) * scale, scale)


def norm_backward(grad, centred, scale, gain):
    scaled = grad * gain
    total = jnp.mean(scaled, axis=1, keepdims=True)
    along = jnp.mean(scaled * centred, axis=1, keepdims=True)
    return scale * (scaled - total - centred * along)


def allowed_mask(segment):
    length = segment.shape[1]
    place = lax.broadcasted_iota(jnp.int32, (length, length), 0)
    other = lax.broadcasted_iota(jnp.int32, (length, length), 1)
    same = segment[:, :, None] == segment[:, None, :]
    return (same & (other <= place)[None])[:, None]


def gelu_value(upper):
    return jax.nn.gelu(upper, approximate=True)


def dot(left, right, dims):
    return lax.dot_general(left, right, (dims, ((), ())), preferred_element_type=f32)


def forward(whole, rows, mask, weights):
    gain1, bias1, w_qkv, b_qv, w_out, b_out, gain2, bias2, w_up, b_up, w_down, b_down = weights
    count = whole.shape[0]
    heads, wide = w_qkv.shape[1:]
    size = wide // 3
    shape4 = (mask.shape[0], mask.shape[2], heads, size)
    factor = 1.0 / math.sqrt(size)
    normed = (norm_parts(whole.astype(f32))[0] * gain1 + bias1).astype(bf16)
    rows = rows.astype(f32)
    centred1, scale1 = norm_parts(rows)
    mixed = jnp.einsum("rd,dhe->rhe", normed, w_qkv, preferred_element_type=f32)
    query = (mixed[..., :size] + b_qv[:, :size]).astype(bf16).reshape(shape4)
    keys = mixed[..., size : 2 * size].astype(bf16).reshape(shape4)
    values = (mixed[..., 2 * size :] + b_qv[:, size:]).astype(bf16).reshape(shape4)
    scores = jnp.einsum("sqhe,skhe->shqk", query, keys, preferred_element_type=f32) * factor
    masked = jnp.where(mask, scores, floor_value)
    raised = jnp.exp(masked - jnp.max(masked, axis=-1, keepdims=True))
    chance = raised / jnp.sum(raised, axis=-1, keepdims=True)
    low = chance.astype(bf16)
    context = jnp.einsum("shqk,skhe->sqhe", low, values, preferred_element_type=f32)
    context = context.reshape(count, heads * size).astype(bf16)
    attn = scatter_rows(dot(context, w_out, ((1,), (0,)))) + b_out
    hidden = rows + attn
    centred2, scale2 = norm_parts(hidden)
    normed2 = gather_rows((centred2 * gain2 + bias2).astype(bf16))
    upper = dot(normed2, w_up, ((1,), (0,))) + b_up
    active = gelu_value(upper).astype(bf16)
    branch = scatter_rows(dot(active, w_down, ((1,), (0,)))) + b_down
    output = (hidden + branch).astype(bf16)
    kept = (
        centred1, scale1, normed, query, keys, values, chance, low, context,
        centred2, scale2, normed2, upper, active,
    )
    return (output, kept)


def backward(grad_whole, grad_rows, weights, kept):
    gain1, bias1, w_qkv, b_qv, w_out, b_out, gain2, bias2, w_up, b_up, w_down, b_down = weights
    (
        centred1, scale1, normed, query, keys, values, chance, low, context,
        centred2, scale2, normed2, upper, active,
    ) = kept
    count = grad_whole.shape[0]
    heads, wide = w_qkv.shape[1:]
    size = wide // 3
    factor = 1.0 / math.sqrt(size)
    grad_out = grad_rows.astype(f32)
    grad_active = dot(grad_whole, w_down, ((1,), (1,)))
    grad_upper = jax.vjp(gelu_value, upper)[1](grad_active)[0].astype(bf16)
    grad_normed2 = scatter_rows(dot(grad_upper, w_up, ((1,), (1,))))
    grad_down = dot(active, grad_whole, ((0,), (0,)))
    grad_up = dot(normed2, grad_upper, ((0,), (0,)))
    grad_hidden = grad_out + norm_backward(grad_normed2, centred2, scale2, gain2)
    grad_attn = grad_hidden.astype(bf16)
    attn_whole = gather_rows(grad_attn)
    grad_context = dot(attn_whole, w_out, ((1,), (1,))).astype(bf16).reshape(query.shape)
    grad_out_w = dot(context, attn_whole, ((0,), (0,)))
    grad_chance = jnp.einsum("sqhe,skhe->shqk", grad_context, values, preferred_element_type=f32)
    delta = jnp.sum(grad_chance * chance, axis=-1, keepdims=True)
    grad_scores = (chance * (grad_chance - delta)).astype(bf16)
    grad_query = (
        jnp.einsum("shqk,skhe->sqhe", grad_scores, keys, preferred_element_type=f32) * factor
    ).astype(bf16)
    grad_keys = (
        jnp.einsum("shqk,sqhe->skhe", grad_scores, query, preferred_element_type=f32) * factor
    ).astype(bf16)
    grad_values = jnp.einsum(
        "shqk,sqhe->skhe", low, grad_context, preferred_element_type=f32
    ).astype(bf16)
    grad_mixed = jnp.concatenate([grad_query, grad_keys, grad_values], axis=-1).reshape(
        count, heads, wide
    )
    grad_normed1 = scatter_rows(
        jnp.einsum("rhe,dhe->rd", grad_mixed, w_qkv, preferred_element_type=f32)
    )
    grad_qkv = jnp.einsum("rd,rhe->dhe", normed, grad_mixed, preferred_element_type=f32)
    grad_qv = jnp.concatenate(
        [
            jnp.sum(grad_query.astype(f32), axis=(0, 1)),
            jnp.sum(grad_values.astype(f32), axis=(0, 1)),
        ],
        axis=-1,
    )
    grad_input = grad_hidden + norm_backward(grad_normed1, centred1, scale1, gain1)
    vectors = (
        jnp.sum(grad_normed1 * centred1, axis=0),
        jnp.sum(grad_normed1, axis=0),
        jnp.sum(grad_attn.astype(f32), axis=0),
        jnp.sum(grad_normed2 * centred2, axis=0),
        jnp.sum(grad_normed2, axis=0),
        jnp.sum(grad_out, axis=0),
    )
    local = (jnp.sum(grad_upper.astype(f32), axis=0), grad_qv)
    return (grad_input.astype(bf16), (grad_qkv, grad_out_w, grad_up, grad_down), vectors, local)


def swap(item):
    return lax.ppermute(item, "section", [(0, 1), (1, 0)])


def body(
    tokens,
    segments,
    cotangent,
    norm1_gain,
    norm1_bias,
    qkv_weight,
    qv_bias,
    out_weight,
    out_bias,
    norm2_gain,
    norm2_bias,
    up_weight,
    up_bias,
    down_weight,
    down_bias,
):
    section = lax.axis_index("section")
    place = lax.axis_index("tensor")
    tensors = lax.axis_size("tensor")
    quads = lax.axis_size("seq")
    first = section == 0
    rows_all, width = tokens.shape
    count = rows_all // 2
    block = count // tensors
    full = width * tensors
    heads, wide = qkv_weight.shape[2:]
    size = wide // 3
    part = norm1_gain.shape[1]
    part_up = up_bias.shape[1]
    part_qv = qv_bias.shape[2]

    def mine(item):
        return lax.dynamic_slice_in_dim(item, section * (item.shape[0] // 2), item.shape[0] // 2, 0)

    def block_of(whole):
        return lax.dynamic_slice_in_dim(whole, place * block, block, 0)

    def columns_of(whole):
        return lax.dynamic_slice_in_dim(whole, place * width, width, 1)

    whole0 = gather_columns(mine(tokens))
    packed = jnp.concatenate(
        [
            norm1_gain[0], norm1_bias[0], out_bias[0], norm2_gain[0], norm2_bias[0], down_bias[0],
            up_bias[0], qv_bias[0].reshape(-1),
        ]
    )
    small = lax.all_gather(packed, ("section", "tensor", "seq"), axis=0, tiled=False)
    small = small.reshape(2, tensors, quads, packed.shape[0]).astype(f32)

    def pair(weight, axis):
        gathered = lax.all_gather(weight, "seq", axis=axis, tiled=True)
        return lax.all_gather(gathered, "section", axis=0, tiled=False)

    w_qkv = pair(qkv_weight[0], 0)
    w_out = pair(out_weight[0].reshape(heads * size, -1), 1)
    w_up = pair(up_weight[0], 0)
    w_down = pair(down_weight[0], 1)
    whole_cot = gather_columns(mine(cotangent))

    def weights_of(layer):
        own = small[layer]
        vectors = [own[:, :, i * part : (i + 1) * part].reshape(full) for i in range(6)]
        local = lax.dynamic_slice_in_dim(own, place, 1, 0)[0]
        b_up = local[:, 6 * part : 6 * part + part_up].reshape(-1)
        b_qv = local[:, 6 * part + part_up :].reshape(quads, heads, part_qv)
        b_qv = jnp.transpose(b_qv, (1, 0, 2)).reshape(heads, 2 * size)
        return (
            vectors[0], vectors[1], w_qkv[layer], b_qv, w_out[layer], vectors[2],
            vectors[3], vectors[4], w_up[layer], b_up, w_down[layer], vectors[5],
        )

    params = (weights_of(0), weights_of(1))
    mask = allowed_mask(mine(segments))
    out0, kept0 = forward(whole0, block_of(whole0), mask, params[0])
    whole1 = gather_rows(out0)
    out1, kept1 = forward(whole1, out0, mask, params[1])
    grad1, big1, vec1, loc1 = backward(whole_cot, block_of(whole_cot), params[1], kept1)

    def reduce_big(big):
        axes = (0, 1, 0, 1)
        return tuple(
            lax.psum_scatter(item.astype(bf16), "seq", scatter_dimension=axis, tiled=True)
            for item, axis in zip(big, axes)
        )

    red1 = reduce_big(big1)
    whole_grad = gather_rows(grad1)
    grad0, big0, vec0, loc0 = backward(whole_grad, grad1, params[0], kept0)
    red0 = reduce_big(big0)

    def to_columns(rows):
        return lax.all_to_all(rows, "tensor", split_axis=1, concat_axis=0, tiled=True)

    def settle(of0, of1):
        own = jnp.where(first, of0, of1)
        other = swap(jnp.where(first, of1, of0))
        return jnp.where(
            first, jnp.concatenate([own, other]), jnp.concatenate([other, own])
        )

    outputs = settle(columns_of(whole1), to_columns(out1))
    input_grads = settle(to_columns(grad0), columns_of(whole_grad))
    totals = tuple(
        jnp.where(first, a, b).astype(f32) + swap(jnp.where(first, b, a)).astype(f32)
        for a, b in zip(red0, red1)
    )

    def pack(vectors, local):
        rows = [item.reshape(tensors, quads, part) for item in vectors]
        up = local[0].reshape(1, quads, part_up)
        qv = jnp.transpose(local[1].reshape(heads, quads, part_qv), (1, 0, 2))
        here = jnp.concatenate([up, qv.reshape(1, quads, heads * part_qv)], axis=-1)
        ours = lax.broadcasted_iota(jnp.int32, (tensors, 1, 1), 0) == place
        rows.append(jnp.where(ours, here, 0.0))
        return jnp.concatenate(rows, axis=-1)

    vectors = jnp.stack([pack(vec0, loc0), pack(vec1, loc1)])
    vectors = vectors.reshape(2 * tensors * quads, -1)
    vectors = lax.psum_scatter(
        vectors, ("section", "tensor", "seq"), scatter_dimension=0, tiled=True
    )[0]
    small_grads = [vectors[i * part : (i + 1) * part] for i in range(6)]
    g_up = vectors[6 * part : 6 * part + part_up]
    g_qv = vectors[6 * part + part_up :].reshape(heads, part_qv)
    result = (
        outputs,
        input_grads,
        small_grads[0],
        small_grads[1],
        totals[0],
        g_qv,
        totals[1].reshape(heads, size, -1),
        small_grads[2],
        small_grads[3],
        small_grads[4],
        totals[2],
        g_up,
        totals[3],
        small_grads[5],
    )
    return tuple(item[None] for item in result)


def solution(mesh):
    return jax.shard_map(
        body,
        mesh=mesh,
        in_specs=(
            P("seq", "tensor"),
            P("seq", None),
            P("seq", "tensor"),
            P("section", ("tensor", "seq")),
            P("section", ("tensor", "seq")),
            P("section", "seq", "tensor", None),
            P("section", "tensor", "seq"),
            P("section", "tensor", None, "seq"),
            P("section", ("tensor", "seq")),
            P("section", ("tensor", "seq")),
            P("section", ("tensor", "seq")),
            P("section", "seq", "tensor"),
            P("section", ("tensor", "seq")),
            P("section", "tensor", "seq"),
            P("section", ("tensor", "seq")),
        ),
        out_specs=(
            P("section", "seq", "tensor"),
            P("section", "seq", "tensor"),
            P("section", ("tensor", "seq")),
            P("section", ("tensor", "seq")),
            P("section", "seq", "tensor", None),
            P("section", "tensor", "seq"),
            P("section", "tensor", None, "seq"),
            P("section", ("tensor", "seq")),
            P("section", ("tensor", "seq")),
            P("section", ("tensor", "seq")),
            P("section", "seq", "tensor"),
            P("section", ("tensor", "seq")),
            P("section", "tensor", "seq"),
            P("section", ("tensor", "seq")),
        ),
        check_vma=False,
    )
```
